32 devices in a mesh: ctx: 4 (over z), ep: 8 (over y, x, core).
Axes of the slice: x: 2, y: 2, z: 4, core: 2. Of those that a mesh axis runs over, the one named last changes fastest.
Arguments:
- hidden_in: bfloat16 [8, 512, 7168], P('ep', None, 'ctx'), may hold values from -6 to 6
- expert_ids: int32 [8, 512, 1], P('ep'), may hold values from 0 to 3; in each aligned block of 512 rows (0 to 511, 512 to 1023, ..., all dimensions but the last counted through in order) at most 192 rows name the same one
- route_weight: float32 [8, 512, 1], P('ep'), may hold values from 0.05 to 1
- w_gate: bfloat16 [7168, 4096], P('ctx', 'ep'), may hold values from -0.0625 to 0.0625
- w_up: bfloat16 [7168, 4096], P('ctx', 'ep'), may hold values from -0.0625 to 0.0625
- w_down: bfloat16 [4096, 7168], P('ep', 'ctx'), may hold values from -0.1875 to 0.1875
- queries: bfloat16 [8, 512, 6912], P('ep', 'ctx'), may hold values from -112 to 112
- latents: bfloat16 [8, 512, 512], P('ep', 'ctx'), may hold values from -5 to 5
- rope_keys: bfloat16 [8, 512, 64], P('ep', 'ctx'), may hold values from -5 to 5
- marks: int32 [8, 512], P('ep', 'ctx'), may hold values from 0 to 1, as said below
Outputs:
- moe_out: bfloat16 [8, 512, 7168], P('ep', None, 'ctx')
- context: bfloat16 [8, 512, 6144], P('ep', 'ctx')
The draws below stay inside these ranges and needn't reach their ends.
Inputs may be any that keep to these rules, and one draw needn't show every extreme that they name: `expert_ids`: in each sequence no expert is named by more than 192 pairs; in some sequences one is named by exactly 192. `marks`: in each sequence the positions marked 1 form one run of consecutive positions, all in the first half.
All inputs are finite; a program needn't handle non-finite values.
Results may differ from the reference program's by a relative error of at most 0.02.
Values may be sent and summed in bfloat16 or wider, within the bound.
A program may use at most 128 MiB of HBM per device.

```python
import math
import jax
import jax.numpy as jnp
import numpy as np
from jax import lax

D = 7168
LAT = 512
ROPE = 64
QK_DIM = 192
HEADS = 12
HID = 1024
TOPK = 1
SEQ = 512
SEQS = 8
EXPERTS = 4
CAP = 192


def attention_parts(key):
    base = jax.random.fold_in(key, 4242)
    query_key, latent_key, rope_key = jax.random.split(base, 3)
    query_shape = (SEQS, SEQ, HEADS, LAT + ROPE)
    query_vals = jnp.clip(jax.random.normal(query_key, query_shape, jnp.float32), -5.0, 5.0)
    latent_vals = jnp.clip(jax.random.normal(latent_key, (SEQS, SEQ, LAT), jnp.float32), -5.0, 5.0)
    rope_vals = jnp.clip(jax.random.normal(rope_key, (SEQS, SEQ, ROPE), jnp.float32), -5.0, 5.0)
    return (query_vals.reshape(SEQS, SEQ, HEADS * (LAT + ROPE)), latent_vals, rope_vals)


def draw_queries(key, part):
    return attention_parts(key)[0].astype(jnp.bfloat16)


def draw_latents(key, part):
    return attention_parts(key)[1].astype(jnp.bfloat16)


def draw_rope_keys(key, part):
    return attention_parts(key)[2].astype(jnp.bfloat16)


def draw_marks(key, part):
    start_key, length_key = jax.random.split(jax.random.fold_in(key, 77))
    quarter = SEQ // 4
    starts = jax.random.randint(start_key, (SEQS, 1), 0, quarter + 1)
    spans = jax.random.randint(length_key, (SEQS, 1), 1, quarter + 1)
    positions = jnp.arange(SEQ, dtype=jnp.int32)[None, :]
    inside = (positions >= starts) & (positions < starts + spans)
    return inside.astype(jnp.int32)


def block_levels(rng, dims, cuts, smallest, high):
    def one(position, parts):
        steps = jax.random.uniform(jax.random.fold_in(jax.random.fold_in(rng, 6), position), (parts,), jnp.float32, smallest / len(cuts), high / len(cuts))
        return jnp.repeat(jnp.exp(steps), dims[position] // parts).reshape((-1,) + (1,) * (len(dims) - position - 1))

    gain = one(*cuts[0])
    for cut in cuts[1:]:
        gain = gain * one(*cut)
    return gain


def assign_block(rng, own, number, rows, count, top, most, slope):
    order = jax.random.permutation(rng, count)
    heavy_load, common = portions_of(count, rows * top, most, slope, True), portions_of(count, rows * top, most, slope, False)
    places = jnp.arange(count)

    def named(tallies, rotation):
        used = int((tallies > 0).sum())
        fixed = max(1, used // 4)
        moved = fixed + (places - fixed + rotation * (used - fixed)) % max(1, count - fixed)
        return jnp.zeros((count,), jnp.int32).at[order[jnp.where(places < fixed, places, moved)]].set(jnp.asarray(tallies, jnp.int32))

    tallies = jnp.where(number % 4 == 0, named(heavy_load, number // 4), named(common, number - number // 4 - 1))
    mixed = jax.random.permutation(jax.random.fold_in(own, 3), count)
    source_of, taker = mixed[0:count // 2 * 2:2], mixed[1:count // 2 * 2:2]
    room = jnp.minimum(tallies[source_of] - 1, most - tallies[taker]) // 2
    room = jnp.where((source_of == order[0]) | (taker == order[0]) | (tallies[taker] == 0), 0, jnp.maximum(room, 0))
    moved = jax.random.randint(jax.random.fold_in(own, 4), (count // 2,), 0, 1 << 20) % (room + 1)
    tallies = tallies.at[source_of].add(-moved).at[taker].add(moved)
    labels = jnp.searchsorted(jnp.cumsum(tallies), jnp.arange(rows * top), side="right").astype(jnp.int32)
    listing = labels.reshape(top, rows).T
    listing = listing[jax.random.permutation(jax.random.fold_in(own, 1), rows)]
    rotation = jax.random.randint(jax.random.fold_in(own, 2), (rows, 1), 0, top)
    return jnp.take_along_axis(listing, (jnp.arange(top)[None, :] + rotation) % top, axis=1)


def portions_of(number_of, total, bound, lean, full):
    portions = [(1 << 20) // math.isqrt(grade ** lean) + 1 for grade in range(1, number_of + 1)]
    largest = bound if full else min(bound, max(-(-total // number_of), total * portions[0] // sum(portions)))
    least = 1 if total - largest >= number_of - 1 else 0
    given, surplus = [largest] + [least] * (number_of - 1), total - largest - least * (number_of - 1)
    while surplus > 0:
        candidates = [i for i in range(1, number_of) if given[i] < largest] or [i for i in range(1, number_of) if given[i] < bound]
        whole, left = sum([portions[i] for i in candidates]), surplus
        for i in candidates:
            extra = min(bound - given[i], max(1, left * portions[i] // whole), surplus)
            given[i] = given[i] + extra
            surplus = surplus - extra
    return np.array(given)


def noise(rng, shape, deviation, reach, pieces=(), kind=jnp.bfloat16):
    values = jax.random.normal(rng, shape, jnp.float32) * deviation
    if len(pieces) > 0:
        values = block_levels(rng, shape, pieces, -0.22, 0.18) * values
    return jnp.clip(values, min=-reach, max=reach).astype(kind)


def setup_inputs(seed: int = 0) -> dict:
    arg_keys = jax.random.split(jax.random.key(seed), 11)
    hidden_in = noise(arg_keys[0], (SEQS, SEQ, D), 1.0, 6.0, ((0, 8), (2, 4)))
    expert_ids_keys = jax.random.split(jax.random.fold_in(arg_keys[1], 1), SEQS * SEQ // SEQ)
    expert_ids_turns = jax.random.permutation(jax.random.fold_in(arg_keys[1], 3), SEQS * SEQ // SEQ)
    expert_ids = jax.vmap(lambda own, number: assign_block(jax.random.fold_in(arg_keys[1], 2), own, number, SEQ, EXPERTS, TOPK, CAP, 2))(expert_ids_keys, expert_ids_turns).reshape((SEQS, SEQ, TOPK))
    route_weight = jnp.clip(jnp.exp(math.log(1.0) - 2.9957323 * jax.random.uniform(arg_keys[2], (SEQS, SEQ, TOPK), jnp.float32) ** block_levels(arg_keys[2], (SEQS, SEQ, TOPK), ((0, 8),), -0.2, 0.2)), 0.05, 1.0)
    w_gate = noise(arg_keys[3], (D, EXPERTS * HID), D ** -0.5, 0.0625, ((0, 4), (1, 8)))
    w_up = noise(arg_keys[4], (D, EXPERTS * HID), D ** -0.5, 0.0625, ((0, 4), (1, 8)))
    w_down = noise(arg_keys[5], (EXPERTS * HID, D), HID ** -0.5, 0.1875, ((0, 8), (1, 4)))
    queries = draw_queries(jax.random.fold_in(arg_keys[10], 71), 0)
    latents = draw_latents(jax.random.fold_in(arg_keys[10], 71), 0)
    rope_keys = draw_rope_keys(jax.random.fold_in(arg_keys[10], 71), 0)
    marks = draw_marks(jax.random.fold_in(arg_keys[10], 71), 0)
    return dict(hidden_in=hidden_in, expert_ids=expert_ids, route_weight=route_weight, w_gate=w_gate, w_up=w_up, w_down=w_down, queries=queries, latents=latents, rope_keys=rope_keys, marks=marks)


def attend_sequence(packed):
    query_all, latent_seq, rope_seq, marks_seq = packed
    length = latent_seq.shape[0]
    query_heads = query_all.reshape(length, HEADS, LAT + ROPE).astype(jnp.float32)
    query_lat = query_heads[:, :, :LAT]
    query_rot = query_heads[:, :, LAT:]
    latent_wide = latent_seq.astype(jnp.float32)
    scores = jnp.einsum('qhd,kd->hqk', query_lat, latent_wide)
    scores = scores + jnp.einsum('qhd,kd->hqk', query_rot, rope_seq.astype(jnp.float32))
    scores = scores * (1.0 / math.sqrt(QK_DIM))
    positions = jnp.arange(length, dtype=jnp.int32)
    own_key = positions[None, :] == positions[:, None]
    visible = (positions[None, :] <= positions[:, None]) & ((marks_seq[None, :] == 0) | own_key)
    masked = jnp.where(visible[None], scores, -jnp.inf)
    highest = lax.optimization_barrier(jnp.max(masked, axis=-1, keepdims=True))
    weights = jnp.exp(masked - highest)
    total = lax.optimization_barrier(jnp.sum(weights, axis=-1))
    rounded = lax.optimization_barrier(weights.astype(jnp.bfloat16)).astype(jnp.float32)
    summed = jnp.einsum('hqk,kd->qhd', rounded, latent_wide)
    result = summed / jnp.transpose(total)[:, :, None]
    return result.reshape(length, HEADS * LAT).astype(jnp.bfloat16)

def reference(hidden_in, expert_ids, route_weight, w_gate, w_up, w_down, queries, latents, rope_keys, marks):
    context = lax.map(attend_sequence, (queries, latents, rope_keys, marks))
    pairs = SEQ * TOPK
    flat_ids = expert_ids.reshape(SEQS, pairs)
    flat_weight = route_weight.reshape(SEQS, pairs)
    slot_range = jnp.arange(CAP, dtype=jnp.int32)
    pair_range = jnp.arange(pairs, dtype=jnp.int32)
    seq_range = jnp.arange(SEQS, dtype=jnp.int32)[:, None]
    half = HID // 2

    def one_expert(expert, total):
        expert_id = jnp.asarray(expert).astype(jnp.int32)
        chosen = flat_ids == expert_id
        rank = jnp.cumsum(chosen.astype(jnp.int32), axis=1) - 1
        match = chosen[:, None, :] & (rank[:, None, :] == slot_range[None, :, None])
        filled = jnp.any(match, axis=-1)
        pair_index = lax.optimization_barrier(jnp.sum(jnp.where(match, pair_range[None, None, :], 0), axis=-1)).astype(jnp.int32)
        token_index = (pair_index // TOPK).astype(jnp.int32)
        gathered = jnp.take_along_axis(hidden_in, token_index[:, :, None], axis=1).reshape(SEQS * CAP, D)
        start = (expert_id * HID).astype(jnp.int32)
        gate_cols = lax.dynamic_slice_in_dim(w_gate, start, HID, 1)
        up_cols = lax.dynamic_slice_in_dim(w_up, start, HID, 1)
        down_rows = lax.dynamic_slice_in_dim(w_down, start, HID, 0)
        gate_act = jnp.dot(gathered, gate_cols, preferred_element_type=jnp.float32)
        up_act = jnp.dot(gathered, up_cols, preferred_element_type=jnp.float32)
        hidden = (jax.nn.silu(gate_act) * up_act).astype(jnp.bfloat16)
        first_half = jnp.dot(hidden[:, :half], down_rows[:half], preferred_element_type=jnp.float32).astype(jnp.bfloat16)
        second_half = jnp.dot(hidden[:, half:], down_rows[half:], preferred_element_type=jnp.float32).astype(jnp.bfloat16)
        combined = (first_half.astype(jnp.float32) + second_half.astype(jnp.float32)).reshape(SEQS, CAP, D)
        slot_weight = jnp.take_along_axis(flat_weight, pair_index, axis=1)
        contribution = jnp.where(filled[:, :, None], slot_weight[:, :, None] * combined, 0.0)
        return total.at[seq_range, token_index].add(contribution)
    moe_sum = lax.fori_loop(0, EXPERTS, one_expert, jnp.zeros((SEQS, SEQ, D), jnp.float32))
    return (moe_sum.astype(jnp.bfloat16), context)
```

```python
import functools
import math

import jax
import jax.numpy as jnp
from jax import lax
from jax.experimental import pallas as pl
from jax.experimental.pallas import tpu as pltpu
from jax.sharding import PartitionSpec as P

LAT = 512
ROPE = 64
QK_DIM = 192
CHUNKS = 8
MESH = pl.DeviceIdType.MESH


def flip(a, b, size):
    out = 0
    step = 1
    while step < size:
        out = out + lax.rem(lax.div(a, step) + lax.div(b, step), 2) * step
        step *= 2
    return out


def expert_kernel(
    chips,
    depth,
    cap,
    group,
    slot_ref,
    feat_ref,
    gate_ref,
    up_ref,
    down_ref,
    kv_ref,
    ret_ref,
    gat_ref,
    packed,
    rows,
    part_out,
    part_in,
    hid,
    half_out,
    half_in,
    summed,
    d_send,
    d_recv,
    f_send,
    f_recv,
    c_send,
    c_recv,
    b_send,
    b_recv,
    h_send,
    h_recv,
    r_send,
    r_recv,
    g_send,
    g_recv,
    l_sem,
):
    me = lax.axis_index("ep")
    z = lax.axis_index("ctx")
    core = lax.rem(me, 2)
    chip = lax.div(me, 2)
    sibling = me + 1 - 2 * core
    width = feat_ref.shape[1]
    hidden = gate_ref.shape[1]
    quarter = hidden // 2
    n = CHUNKS
    block_rows = group * cap

    def block(buf, source):
        if group == 1:
            return buf.at[source]
        start = pl.multiple_of(lax.rem(source, group) * cap, cap)
        return buf.at[lax.div(source, group), pl.ds(start, cap)]

    def remote(src, dst, send, recv, **device):
        return pltpu.make_async_remote_copy(
            src_ref=src, dst_ref=dst, send_sem=send, recv_sem=recv,
            device_id=device, device_id_type=MESH,
        )

    def dispatch(j):
        return remote(packed.at[j], block(rows, me), d_send.at[j], d_recv.at[chip], ep=2 * j + core)

    def arrival(j):
        return remote(packed.at[j], block(rows, 2 * j + core), d_send.at[j], d_recv.at[j], ep=2 * j + core)

    def forward(s):
        j = lax.div(s, 2)
        return remote(block(rows, s), block(rows, s), f_send.at[j], f_recv.at[j], ep=sibling)

    nexts = (z + 1, z - 1)
    prevs = (z - 1, z + 1)
    places = (z, depth - 1 - z)

    def chain(d, t):
        at = d * n + t
        return remote(part_out.at[at], part_in.at[at], c_send.at[at], c_recv.at[at], ctx=nexts[d])

    def spread(d, t):
        at = d * n + t
        return remote(hid.at[at], hid.at[at], b_send.at[at], b_recv.at[at], ctx=prevs[d])

    def swap(s):
        j = lax.div(s, 2)
        return remote(block(half_out, s), half_in.at[j], h_send.at[j], h_recv.at[j], ep=sibling)

    def back(j):
        return remote(summed.at[j], ret_ref.at[chip], r_send.at[j], r_recv.at[chip], ep=2 * j + core)

    def home(j):
        return remote(summed.at[j], ret_ref.at[j], r_send.at[j], r_recv.at[j], ep=2 * j + core)

    def share(o):
        other = lax.rem(z + o, depth)
        return remote(kv_ref, gat_ref.at[z], g_send.at[o], g_recv.at[o], ctx=other)

    def shared(o):
        other = lax.rem(z + depth - o, depth)
        return remote(kv_ref, gat_ref.at[other], g_send.at[o], g_recv.at[o], ctx=other)

    barrier = pltpu.get_barrier_semaphore()

    def greet(o, carry):
        pl.semaphore_signal(
            barrier, inc=1, device_id={"ep": 2 * flip(chip, o, chips) + core}, device_id_type=MESH
        )
        return carry

    lax.fori_loop(1, chips, greet, 0)
    pl.semaphore_signal(barrier, inc=1, device_id={"ep": sibling}, device_id_type=MESH)
    for o in range(1, depth):
        pl.semaphore_signal(
            barrier, inc=1, device_id={"ctx": lax.rem(z + o, depth)}, device_id_type=MESH
        )
    pl.semaphore_wait(barrier, chips + depth - 1)

    own_kv = pltpu.make_async_copy(kv_ref, gat_ref.at[z], l_sem.at[0])
    own_kv.start()

    slots = slot_ref[...]
    tokens = slots.shape[1]

    def pack(o, carry):
        j = flip(chip, o, chips)
        index = j * cap + lax.broadcasted_iota(jnp.int32, (cap, tokens), 0)
        pick = jnp.where(index == slots, 1.0, 0.0).astype(jnp.bfloat16)
        chosen = jnp.dot(pick, feat_ref[...], preferred_element_type=jnp.float32)
        packed[j] = chosen.astype(jnp.bfloat16)

        @pl.when(o < chips)
        def _():
            dispatch(j).start()

        return carry

    lax.fori_loop(1, chips, pack, 0)
    index = chip * cap + lax.broadcasted_iota(jnp.int32, (cap, tokens), 0)
    pick = jnp.where(index == slots, 1.0, 0.0).astype(jnp.bfloat16)
    chosen = jnp.dot(pick, feat_ref[...], preferred_element_type=jnp.float32)
    block(rows, me)[...] = chosen.astype(jnp.bfloat16)

    first = lax.div(me, group)
    lag = depth - 1

    def step(i, carry):
        @pl.when(i < n)
        def _():
            q = flip(first, i, n)
            for g in range(group):
                s = q * group + g
                j = lax.div(s, 2)
                mine = lax.rem(s, 2) == core

                @pl.when(mine & (j != chip))
                def _():
                    arrival(j).wait_recv()

                @pl.when(mine)
                def _():
                    forward(s).start()

            for g in range(group):
                s = q * group + g

                @pl.when(lax.rem(s, 2) != core)
                def _():
                    forward(s).wait_recv()

        for d in range(2):
            t = i - places[d]
            lo, hi = d * quarter, (d + 1) * quarter

            @pl.when((t >= 0) & (t < n))
            def _():
                q = flip(first, t, n)
                at = d * n + t
                x = rows[q]
                gate = jnp.dot(x, gate_ref[:, lo:hi], preferred_element_type=jnp.float32)
                up = jnp.dot(x, up_ref[:, lo:hi], preferred_element_type=jnp.float32)

                @pl.when(places[d] == 0)
                def _():
                    part_out[at, :, :quarter] = gate.astype(jnp.bfloat16)
                    part_out[at, :, quarter:] = up.astype(jnp.bfloat16)
                    chain(d, t).start()

                @pl.when(places[d] > 0)
                def _():
                    chain(d, t).wait_recv()
                    gate_sum = gate + part_in[at, :, :quarter].astype(jnp.float32)
                    up_sum = up + part_in[at, :, quarter:].astype(jnp.float32)

                    @pl.when(places[d] < depth - 1)
                    def _():
                        part_out[at, :, :quarter] = gate_sum.astype(jnp.bfloat16)
                        part_out[at, :, quarter:] = up_sum.astype(jnp.bfloat16)
                        chain(d, t).start()

                    @pl.when(places[d] == depth - 1)
                    def _():
                        hid[at] = (jax.nn.silu(gate_sum) * up_sum).astype(jnp.bfloat16)
                        spread(d, t).start()

        for d in range(2):
            t = i - lag - (depth - 1 - places[d])

            @pl.when((t >= 0) & (t < n) & (places[d] < depth - 1))
            def _():
                spread(d, t).wait_recv()

                @pl.when(places[d] > 0)
                def _():
                    spread(d, t).start()

        t = i - 2 * lag

        @pl.when((t >= 0) & (t < n))
        def _():
            q = flip(first, t, n)
            h0 = hid[t]
            h1 = hid[n + t]
            tile = 256
            for w in range(0, width, tile):
                got = jnp.dot(h0, down_ref[:quarter, w:w + tile], preferred_element_type=jnp.float32)
                got = got + jnp.dot(
                    h1, down_ref[quarter:, w:w + tile], preferred_element_type=jnp.float32
                )
                half_out[q, :, w:w + tile] = got.astype(jnp.bfloat16)
            for g in range(group):
                s = q * group + g

                @pl.when(lax.rem(s, 2) != core)
                def _():
                    swap(s).start()

        t2 = i - 2 * lag - 1

        @pl.when((t2 >= 0) & (t2 < n))
        def _():
            q = flip(first, t2, n)
            for g in range(group):
                s = q * group + g
                j = lax.div(s, 2)

                @pl.when(lax.rem(s, 2) == core)
                def _():
                    swap(s).wait_recv()
                    total = block(half_out, s)[...].astype(jnp.float32)
                    total = total + half_in[j].astype(jnp.float32)
                    summed[j] = total.astype(jnp.bfloat16)

                    @pl.when(j != chip)
                    def _():
                        back(j).start()

                    @pl.when(j == chip)
                    def _():
                        pltpu.make_async_copy(summed.at[j], ret_ref.at[j], l_sem.at[1]).start()

        @pl.when(i == n + lag)
        def _():
            for o in range(1, depth):
                share(o).start()

        return carry

    lax.fori_loop(0, n + 2 * lag + 1, step, 0)

    def finish(o, carry):
        j = flip(chip, o, chips)
        dispatch(j).wait_send()
        back(j).wait_send()
        home(j).wait_recv()
        return carry

    lax.fori_loop(1, chips, finish, 0)

    def finish_core(j, carry):
        forward(2 * j + core).wait_send()
        swap(2 * j + 1 - core).wait_send()
        return carry

    lax.fori_loop(0, chips, finish_core, 0)

    def finish_chain(t, carry):
        for d in range(2):
            @pl.when(places[d] < depth - 1)
            def _():
                chain(d, t).wait_send()

            @pl.when(places[d] > 0)
            def _():
                spread(d, t).wait_send()

        return carry

    lax.fori_loop(0, n, finish_chain, 0)
    for o in range(1, depth):
        share(o).wait_send()
        shared(o).wait_recv()
    own_kv.wait()
    pltpu.make_async_copy(summed.at[chip], ret_ref.at[chip], l_sem.at[1]).wait()


def expert_call(slots, features, w_gate, w_up, w_down, kv, chips, depth, cap):
    seq_len, width = features.shape
    hidden = w_gate.shape[1]
    group = 2 * chips // CHUNKS
    n = CHUNKS
    tall = group * cap
    dma = pltpu.SemaphoreType.DMA
    bf16 = jnp.bfloat16
    vmem = pl.BlockSpec(memory_space=pltpu.VMEM)
    return pl.pallas_call(
        functools.partial(expert_kernel, chips, depth, cap, group),
        out_shape=(
            jax.ShapeDtypeStruct((chips, cap, width), bf16),
            jax.ShapeDtypeStruct((depth,) + kv.shape, bf16),
        ),
        in_specs=[vmem] * 6,
        out_specs=(pl.BlockSpec(memory_space=pl.ANY), pl.BlockSpec(memory_space=pl.ANY)),
        scratch_shapes=[
            pltpu.VMEM((chips, cap, width), bf16),
            pltpu.VMEM((n, tall, width), bf16),
            pltpu.VMEM((2 * n, tall, hidden), bf16),
            pltpu.VMEM((2 * n, tall, hidden), bf16),
            pltpu.VMEM((2 * n, tall, hidden // 2), bf16),
            pltpu.VMEM((n, tall, width), bf16),
            pltpu.VMEM((chips, cap, width), bf16),
            pltpu.VMEM((chips, cap, width), bf16),
            dma((chips,)), dma((chips,)),
            dma((chips,)), dma((chips,)),
            dma((2 * n,)), dma((2 * n,)),
            dma((2 * n,)), dma((2 * n,)),
            dma((chips,)), dma((chips,)),
            dma((chips,)), dma((chips,)),
            dma((depth,)), dma((depth,)),
            dma((2,)),
        ],
        compiler_params=pltpu.CompilerParams(
            collective_id=0, has_side_effects=True, vmem_limit_bytes=58 << 20
        ),
    )(slots, features, w_gate, w_up, w_down, kv)


def attend(queries, keys, query_pos):
    query_rows = queries.shape[0]
    width = LAT + ROPE
    heads = queries.shape[1] // width
    query_heads = queries.reshape(query_rows, heads, width)
    scale = 1.0 / math.sqrt(QK_DIM)
    latents = keys[:, :LAT]
    marks = keys[:, width]
    key_pos = jnp.arange(keys.shape[0], dtype=jnp.int32)
    scores = jnp.einsum(
        "qhd,kd->hqk", query_heads, keys[:, :width], preferred_element_type=jnp.float32
    )
    scores = scores * scale
    own_key = key_pos[None, :] == query_pos[:, None]
    visible = (key_pos[None, :] <= query_pos[:, None]) & ((marks[None, :] < 0.5) | own_key)
    masked = jnp.where(visible[None], scores, -1e30)
    top = jnp.max(masked, axis=-1)
    weights = jnp.where(visible[None], jnp.exp(masked - top[:, :, None]), 0.0)
    total = jnp.sum(weights, axis=-1)
    acc = jnp.einsum(
        "hqk,kd->hqd", weights.astype(jnp.bfloat16), latents, preferred_element_type=jnp.float32
    )
    result = acc / total[:, :, None]
    result = jnp.transpose(result, (1, 0, 2)).reshape(query_rows, heads * LAT)
    return result.astype(jnp.bfloat16)


def per_device(
    hidden_in, expert_ids, route_weight, w_gate, w_up, w_down, queries, latents, rope_keys, marks
):
    features = hidden_in[0]
    seq_len = features.shape[0]
    slots_per = expert_ids.shape[2]
    chips = lax.axis_size("ep") // 2
    depth = lax.axis_size("ctx")
    capacity = max(2, 3 * seq_len * slots_per // (2 * chips))
    cap = -(-capacity // 16) * 16
    flat_ids = expert_ids[0].reshape(-1)
    onehot = (flat_ids[:, None] == jnp.arange(chips, dtype=jnp.int32)[None, :]).astype(jnp.int32)
    rank = jnp.sum(jnp.cumsum(onehot, axis=0) * onehot, axis=1) - 1
    slot = flat_ids * cap + rank
    query_rows = queries.shape[1]
    lanes = -(-(LAT + ROPE + 1) // 128) * 128
    kv = jnp.concatenate(
        [
            latents[0],
            rope_keys[0],
            jnp.broadcast_to(
                marks[0].astype(jnp.bfloat16)[:, None], (query_rows, lanes - LAT - ROPE)
            ),
        ],
        axis=1,
    )
    ret, gathered = expert_call(
        slot[None, :], features, w_gate, w_up, w_down, kv, chips, depth, cap
    )
    ret = ret.reshape(chips * cap, features.shape[1])
    pick = (slot[:, None] == jnp.arange(chips * cap, dtype=jnp.int32)[None, :]).astype(jnp.bfloat16)
    moe = jnp.dot(pick, ret, preferred_element_type=jnp.float32) * route_weight[0]
    moe = moe.astype(jnp.bfloat16)[None]
    query_pos = lax.axis_index("ctx") * query_rows + jnp.arange(query_rows, dtype=jnp.int32)
    context = attend(queries[0], gathered.reshape(-1, lanes), query_pos)[None]
    return (moe, context)


def solution(mesh):
    placed = (
        P("ep", None, "ctx"),
        P("ep", None, None),
        P("ep", None, None),
        P("ctx", "ep"),
        P("ctx", "ep"),
        P("ep", "ctx"),
        P("ep", "ctx", None),
        P("ep", "ctx", None),
        P("ep", "ctx", None),
        P("ep", "ctx"),
    )
    return jax.shard_map(
        per_device,
        mesh=mesh,
        in_specs=placed,
        out_specs=(P("ep", None, "ctx"), P("ep", "ctx", None)),
        check_vma=False,
    )
```

```python
import functools
import math

import jax
import jax.numpy as jnp
from jax import lax
from jax.experimental import pallas as pl
from jax.experimental.pallas import tpu as pltpu
from jax.sharding import PartitionSpec as P

LAT = 512
ROPE = 64
QK_DIM = 192
CHUNKS = 8
MESH = pl.DeviceIdType.MESH


def flip(a, b, size):
    out = 0
    step = 1
    while step < size:
        out = out + lax.rem(lax.div(a, step) + lax.div(b, step), 2) * step
        step *= 2
    return out


def expert_kernel(
    chips,
    depth,
    cap,
    group,
    ids_ref,
    feat_ref,
    weight_ref,
    gate_ref,
    up_ref,
    down_ref,
    query_ref,
    lat_ref,
    rope_ref,
    mark_ref,
    moe_ref,
    ctx_ref,
    gat_ref,
    ret_ref,
    keys_ref,
    seen_ref,
    packed,
    rows,
    part_out,
    part_in,
    hid,
    half_out,
    half_in,
    summed,
    d_send,
    d_recv,
    f_send,
    f_recv,
    c_send,
    c_recv,
    b_send,
    b_recv,
    h_send,
    h_recv,
    r_send,
    r_recv,
    g_send,
    g_recv,
):
    me = lax.axis_index("ep")
    z = lax.axis_index("ctx")
    core = lax.rem(me, 2)
    chip = lax.div(me, 2)
    sibling = me + 1 - 2 * core
    width = feat_ref.shape[1]
    hidden = gate_ref.shape[1]
    quarter = hidden // 2
    n = CHUNKS
    block_rows = group * cap

    def block(buf, source):
        if group == 1:
            return buf.at[source]
        start = pl.multiple_of(lax.rem(source, group) * cap, cap)
        return buf.at[lax.div(source, group), pl.ds(start, cap)]

    def remote(src, dst, send, recv, **device):
        return pltpu.make_async_remote_copy(
            src_ref=src, dst_ref=dst, send_sem=send, recv_sem=recv,
            device_id=device, device_id_type=MESH,
        )

    def dispatch(j):
        return remote(packed.at[j], block(rows, me), d_send.at[j], d_recv.at[chip], ep=2 * j + core)

    def arrival(j):
        return remote(packed.at[j], block(rows, 2 * j + core), d_send.at[j], d_recv.at[j], ep=2 * j + core)

    def forward(s):
        j = lax.div(s, 2)
        return remote(block(rows, s), block(rows, s), f_send.at[j], f_recv.at[j], ep=sibling)

    nexts = (z + 1, z - 1)
    prevs = (z - 1, z + 1)
    places = (z, depth - 1 - z)

    def chain(d, t):
        at = d * n + t
        return remote(part_out.at[at], part_in.at[at], c_send.at[at], c_recv.at[at], ctx=nexts[d])

    def spread(d, t):
        at = d * n + t
        return remote(hid.at[at], hid.at[at], b_send.at[at], b_recv.at[at], ctx=prevs[d])

    def swap(s):
        j = lax.div(s, 2)
        return remote(block(half_out, s), half_in.at[j], h_send.at[j], h_recv.at[j], ep=sibling)

    def back(j):
        return remote(summed.at[j], ret_ref.at[chip], r_send.at[j], r_recv.at[chip], ep=2 * j + core)

    def home(j):
        return remote(summed.at[j], ret_ref.at[j], r_send.at[j], r_recv.at[j], ep=2 * j + core)

    def share(o):
        other = lax.rem(z + o, depth)
        return remote(gat_ref.at[z], gat_ref.at[z], g_send.at[o], g_recv.at[o], ctx=other)

    def shared(o):
        other = lax.rem(z + depth - o, depth)
        return remote(gat_ref.at[z], gat_ref.at[other], g_send.at[o], g_recv.at[o], ctx=other)

    barrier = pltpu.get_barrier_semaphore()

    def greet(o, carry):
        pl.semaphore_signal(
            barrier, inc=1, device_id={"ep": 2 * flip(chip, o, chips) + core}, device_id_type=MESH
        )
        return carry

    lax.fori_loop(1, chips, greet, 0)
    pl.semaphore_signal(barrier, inc=1, device_id={"ep": sibling}, device_id_type=MESH)
    for o in range(1, depth):
        pl.semaphore_signal(
            barrier, inc=1, device_id={"ctx": lax.rem(z + o, depth)}, device_id_type=MESH
        )

    bf16, f32 = jnp.bfloat16, jnp.float32
    iota = lax.broadcasted_iota
    query_rows = query_ref.shape[0]
    lanes = gat_ref.shape[2]
    width_k = LAT + ROPE
    eye = iota(jnp.int32, (query_rows, query_rows), 0) == iota(jnp.int32, (query_rows, query_rows), 1)
    mark_col = jnp.sum(jnp.where(eye, mark_ref[...].astype(f32), 0.0), axis=1, keepdims=True)
    gat_ref[z, :, :LAT] = lat_ref[...]
    gat_ref[z, :, LAT:width_k] = rope_ref[...]
    gat_ref[z, :, width_k:] = jnp.broadcast_to(mark_col, (query_rows, lanes - width_k)).astype(bf16)

    ids = ids_ref[...]
    tokens = ids.shape[1]
    kinds = max(chips, 16)
    named = iota(jnp.int32, (kinds, tokens), 0) == ids
    earlier = iota(jnp.int32, (tokens, tokens), 0) < iota(jnp.int32, (tokens, tokens), 1)
    counts = jnp.dot(
        jnp.where(named, 1.0, 0.0).astype(bf16),
        jnp.where(earlier, 1.0, 0.0).astype(bf16),
        preferred_element_type=f32,
    )
    rank = jnp.sum(jnp.where(named, counts, 0.0), axis=0, keepdims=True)
    slots = ids * cap + rank.astype(jnp.int32)

    pl.semaphore_wait(barrier, chips + depth - 1)
    for o in range(1, depth):
        share(o).start()

    def pack(o, carry):
        j = flip(chip, o, chips)
        index = j * cap + lax.broadcasted_iota(jnp.int32, (cap, tokens), 0)
        pick = jnp.where(index == slots, 1.0, 0.0).astype(jnp.bfloat16)
        chosen = jnp.dot(pick, feat_ref[...], preferred_element_type=jnp.float32)
        packed[j] = chosen.astype(jnp.bfloat16)

        dispatch(j).start()
        return carry

    lax.fori_loop(1, chips, pack, 0)
    index = chip * cap + lax.broadcasted_iota(jnp.int32, (cap, tokens), 0)
    pick = jnp.where(index == slots, 1.0, 0.0).astype(jnp.bfloat16)
    chosen = jnp.dot(pick, feat_ref[...], preferred_element_type=jnp.float32)
    block(rows, me)[...] = chosen.astype(jnp.bfloat16)

    first = lax.div(me, group)
    lag = depth - 1

    heads = query_ref.shape[1] // width_k
    scale = 1.0 / math.sqrt(QK_DIM)

    def prepare():
        for o in range(1, depth):
            shared(o).wait_recv()
        count = depth * query_rows
        keys = gat_ref[...].reshape(count, lanes)
        row = iota(jnp.int32, (lanes, lanes), 0)
        column = iota(jnp.int32, (lanes, lanes), 1)
        even = (row == column) & (row < width_k)
        odd = row == column + (lanes - width_k)
        contract = (((1,), (1,)), ((), ()))
        for a, chosen in ((0, even), (1, odd)):
            pick = jnp.where(chosen, 1.0, 0.0).astype(bf16)
            keys_ref[a] = lax.dot_general(
                pick, keys, contract, preferred_element_type=f32
            ).astype(bf16)
        pick = jnp.where(iota(jnp.int32, (16, lanes), 1) == width_k, 1.0, 0.0).astype(bf16)
        marks = lax.dot_general(pick, keys, contract, preferred_element_type=f32)[:1]
        query_pos = z * query_rows + iota(jnp.int32, (query_rows, count), 0)
        key_pos = iota(jnp.int32, (query_rows, count), 1)
        visible = (key_pos == query_pos) | ((key_pos < query_pos) & (marks < 0.5))
        seen_ref[...] = jnp.where(visible, 0.0, -1e30)

    def attend_pair(pair):
        latents = gat_ref[:, :, :LAT].reshape(depth * query_rows, LAT)
        base = pl.multiple_of(pair * (2 * width_k), 128)
        mask = seen_ref[...]
        for a in range(2):
            shift = a * (2 * width_k - lanes)
            q = query_ref[:, pl.ds(pl.multiple_of(base + shift, 128), lanes)]
            scores = jnp.dot(q, keys_ref[a], preferred_element_type=f32) * scale
            masked = jnp.where(mask < 0.0, -1e30, scores)
            top = jnp.max(masked, axis=1, keepdims=True)
            weight = jnp.where(mask < 0.0, 0.0, jnp.exp(masked - top))
            total = jnp.sum(weight, axis=1, keepdims=True)
            acc = jnp.dot(weight.astype(bf16), latents, preferred_element_type=f32)
            where = pl.multiple_of((2 * pair + a) * LAT, 128)
            ctx_ref[:, pl.ds(where, LAT)] = (acc / total).astype(bf16)

    def step(i, carry):
        @pl.when(i == 1)
        def _():
            prepare()

        @pl.when((i >= 2) & (i < 2 + heads // 2))
        def _():
            attend_pair(i - 2)

        @pl.when(i < n)
        def _():
            q = flip(first, i, n)
            for g in range(group):
                s = q * group + g
                j = lax.div(s, 2)
                mine = lax.rem(s, 2) == core

                @pl.when(mine & (j != chip))
                def _():
                    arrival(j).wait_recv()

                @pl.when(mine)
                def _():
                    forward(s).start()

            for g in range(group):
                s = q * group + g

                @pl.when(lax.rem(s, 2) != core)
                def _():
                    forward(s).wait_recv()

        for d in range(2):
            t = i - places[d]
            lo, hi = d * quarter, (d + 1) * quarter

            @pl.when((t >= 0) & (t < n))
            def _():
                q = flip(first, t, n)
                at = d * n + t
                x = rows[q]
                gate = jnp.dot(x, gate_ref[:, lo:hi], preferred_element_type=jnp.float32)
                up = jnp.dot(x, up_ref[:, lo:hi], preferred_element_type=jnp.float32)

                @pl.when(places[d] == 0)
                def _():
                    part_out[at, :, :quarter] = gate.astype(jnp.bfloat16)
                    part_out[at, :, quarter:] = up.astype(jnp.bfloat16)
                    chain(d, t).start()

                @pl.when(places[d] > 0)
                def _():
                    chain(d, t).wait_recv()
                    gate_sum = gate + part_in[at, :, :quarter].astype(jnp.float32)
                    up_sum = up + part_in[at, :, quarter:].astype(jnp.float32)

                    @pl.when(places[d] < depth - 1)
                    def _():
                        part_out[at, :, :quarter] = gate_sum.astype(jnp.bfloat16)
                        part_out[at, :, quarter:] = up_sum.astype(jnp.bfloat16)
                        chain(d, t).start()

                    @pl.when(places[d] == depth - 1)
                    def _():
                        hid[at] = (jax.nn.silu(gate_sum) * up_sum).astype(jnp.bfloat16)
                        spread(d, t).start()

        for d in range(2):
            t = i - lag - (depth - 1 - places[d])

            @pl.when((t >= 0) & (t < n) & (places[d] < depth - 1))
            def _():
                spread(d, t).wait_recv()

                @pl.when(places[d] > 0)
                def _():
                    spread(d, t).start()

        t = i - 2 * lag

        @pl.when((t >= 0) & (t < n))
        def _():
            q = flip(first, t, n)
            h0 = hid[t]
            h1 = hid[n + t]
            tile = 256
            for w in range(0, width, tile):
                got = jnp.dot(h0, down_ref[:quarter, w:w + tile], preferred_element_type=jnp.float32)
                got = got + jnp.dot(
                    h1, down_ref[quarter:, w:w + tile], preferred_element_type=jnp.float32
                )
                half_out[q, :, w:w + tile] = got.astype(jnp.bfloat16)
            for g in range(group):
                s = q * group + g

                @pl.when(lax.rem(s, 2) != core)
                def _():
                    swap(s).start()

        t2 = i - 2 * lag - 1

        @pl.when((t2 >= 0) & (t2 < n))
        def _():
            q = flip(first, t2, n)
            for g in range(group):
                s = q * group + g
                j = lax.div(s, 2)

                @pl.when(lax.rem(s, 2) == core)
                def _():
                    swap(s).wait_recv()
                    total = block(half_out, s)[...].astype(jnp.float32)
                    total = total + half_in[j].astype(jnp.float32)
                    summed[j] = total.astype(jnp.bfloat16)

                    @pl.when(j != chip)
                    def _():
                        back(j).start()

                    @pl.when(j == chip)
                    def _():
                        ret_ref[j] = total.astype(jnp.bfloat16)

        return carry

    lax.fori_loop(0, max(n + 2 * lag + 1, 2 + heads // 2), step, 0)

    def land(o, carry):
        home(flip(chip, o, chips)).wait_recv()
        return carry

    lax.fori_loop(1, chips, land, 0)
    diagonal = iota(jnp.int32, (tokens, tokens), 0) == iota(jnp.int32, (tokens, tokens), 1)
    slot_col = jnp.sum(jnp.where(diagonal, slots, 0), axis=1, keepdims=True)
    pick = jnp.where(iota(jnp.int32, (tokens, chips * cap), 1) == slot_col, 1.0, 0.0).astype(bf16)
    tile = 256
    for w in range(0, width, tile):
        mixed = jnp.dot(
            pick,
            ret_ref[:, :, w:w + tile].reshape(chips * cap, tile),
            preferred_element_type=f32,
        )
        moe_ref[:, w:w + tile] = (mixed * weight_ref[...]).astype(bf16)

    def finish(o, carry):
        j = flip(chip, o, chips)
        dispatch(j).wait_send()
        back(j).wait_send()
        return carry

    lax.fori_loop(1, chips, finish, 0)

    def finish_core(j, carry):
        forward(2 * j + core).wait_send()
        swap(2 * j + 1 - core).wait_send()
        return carry

    lax.fori_loop(0, chips, finish_core, 0)

    def finish_chain(t, carry):
        for d in range(2):
            @pl.when(places[d] < depth - 1)
            def _():
                chain(d, t).wait_send()

            @pl.when(places[d] > 0)
            def _():
                spread(d, t).wait_send()

        return carry

    lax.fori_loop(0, n, finish_chain, 0)
    for o in range(1, depth):
        share(o).wait_send()


def expert_call(ids, features, weight, w_gate, w_up, w_down, queries, latents, ropes, marks, chips, depth, cap):
    seq_len, width = features.shape
    hidden = w_gate.shape[1]
    group = 2 * chips // CHUNKS
    n = CHUNKS
    tall = group * cap
    query_rows = queries.shape[0]
    heads = queries.shape[1] // (LAT + ROPE)
    lanes = -(-(LAT + ROPE + 1) // 128) * 128
    dma = pltpu.SemaphoreType.DMA
    bf16 = jnp.bfloat16
    vmem = pl.BlockSpec(memory_space=pltpu.VMEM)
    return pl.pallas_call(
        functools.partial(expert_kernel, chips, depth, cap, group),
        out_shape=(
            jax.ShapeDtypeStruct((seq_len, width), bf16),
            jax.ShapeDtypeStruct((query_rows, heads * LAT), bf16),
        ),
        in_specs=[vmem] * 10,
        out_specs=(vmem, vmem),
        scratch_shapes=[
            pltpu.VMEM((depth, query_rows, lanes), bf16),
            pltpu.VMEM((chips, cap, width), bf16),
            pltpu.VMEM((2, lanes, depth * query_rows), bf16),
            pltpu.VMEM((query_rows, depth * query_rows), jnp.float32),
            pltpu.VMEM((chips, cap, width), bf16),
            pltpu.VMEM((n, tall, width), bf16),
            pltpu.VMEM((2 * n, tall, hidden), bf16),
            pltpu.VMEM((2 * n, tall, hidden), bf16),
            pltpu.VMEM((2 * n, tall, hidden // 2), bf16),
            pltpu.VMEM((n, tall, width), bf16),
            pltpu.VMEM((chips, cap, width), bf16),
            pltpu.VMEM((chips, cap, width), bf16),
            dma((chips,)), dma((chips,)),
            dma((chips,)), dma((chips,)),
            dma((2 * n,)), dma((2 * n,)),
            dma((2 * n,)), dma((2 * n,)),
            dma((chips,)), dma((chips,)),
            dma((chips,)), dma((chips,)),
            dma((depth,)), dma((depth,)),
        ],
        compiler_params=pltpu.CompilerParams(
            collective_id=0, has_side_effects=True, vmem_limit_bytes=60 << 20
        ),
    )(ids, features, weight, w_gate, w_up, w_down, queries, latents, ropes, marks)


def per_device(
    hidden_in, expert_ids, route_weight, w_gate, w_up, w_down, queries, latents, rope_keys, marks
):
    features = hidden_in[0]
    seq_len = features.shape[0]
    slots_per = expert_ids.shape[2]
    chips = lax.axis_size("ep") // 2
    depth = lax.axis_size("ctx")
    capacity = max(2, 3 * seq_len * slots_per // (2 * chips))
    cap = -(-capacity // 16) * 16
    moe, context = expert_call(
        expert_ids[0].reshape(1, -1),
        features,
        route_weight[0],
        w_gate,
        w_up,
        w_down,
        queries[0],
        latents[0],
        rope_keys[0],
        marks,
        chips,
        depth,
        cap,
    )
    return (moe[None], context[None])


def solution(mesh):
    placed = (
        P("ep", None, "ctx"),
        P("ep", None, None),
        P("ep", None, None),
        P("ctx", "ep"),
        P("ctx", "ep"),
        P("ep", "ctx"),
        P("ep", "ctx", None),
        P("ep", "ctx", None),
        P("ep", "ctx", None),
        P("ep", "ctx"),
    )
    return jax.shard_map(
        per_device,
        mesh=mesh,
        in_specs=placed,
        out_specs=(P("ep", None, "ctx"), P("ep", "ctx", None)),
        check_vma=False,
    )
```

```python
import functools
import math

import jax
import jax.numpy as jnp
from jax import lax
from jax.experimental import pallas as pl
from jax.experimental.pallas import tpu as pltpu
from jax.sharding import PartitionSpec as P

LAT = 512
ROPE = 64
QK_DIM = 192
CHUNKS = 16
FAR = 4
LAG = 2
MESH = pl.DeviceIdType.MESH


def flip(a, b, size):
    out = 0
    step = 1
    while step < size:
        out = out + lax.rem(lax.div(a, step) + lax.div(b, step), 2) * step
        step *= 2
    return out


def expert_kernel(
    chips,
    depth,
    cap,
    split,
    group,
    ids_ref,
    feat_ref,
    weight_ref,
    gate_ref,
    up_ref,
    down_ref,
    query_ref,
    lat_ref,
    rope_ref,
    mark_ref,
    moe_ref,
    ctx_ref,
    gat_ref,
    ret_ref,
    keys_ref,
    seen_ref,
    packed,
    rows,
    part_out,
    part_in,
    hid,
    half_out,
    half_in,
    summed,
    d_send,
    d_recv,
    f_send,
    f_recv,
    c_send,
    c_recv,
    b_send,
    b_recv,
    h_send,
    h_recv,
    r_send,
    r_recv,
    g_send,
    g_recv,
):
    me = lax.axis_index("ep")
    z = lax.axis_index("ctx")
    core = lax.rem(me, 2)
    chip = lax.div(me, 2)
    sibling = me + 1 - 2 * core
    width = feat_ref.shape[1]
    hidden = gate_ref.shape[1]
    quarter = hidden // 2
    n = CHUNKS
    unit = cap // split

    def block(buf, v):
        if group == 1:
            return buf.at[v]
        start = pl.multiple_of(lax.rem(v, group) * unit, unit)
        return buf.at[lax.div(v, group), pl.ds(start, unit)]

    def pair_of(v):
        return lax.div(v, 2 * split) * split + lax.rem(v, split)

    def core_of(v):
        return lax.rem(lax.div(v, split), 2)

    def remote(src, dst, send, recv, **device):
        return pltpu.make_async_remote_copy(
            src_ref=src, dst_ref=dst, send_sem=send, recv_sem=recv,
            device_id=device, device_id_type=MESH,
        )

    def peer(m):
        return 2 * lax.div(m, split) + core

    def dispatch(m):
        h = lax.rem(m, split)
        return remote(
            packed.at[m], block(rows, me * split + h), d_send.at[m], d_recv.at[chip * split + h], ep=peer(m)
        )

    def arrival(m):
        v = peer(m) * split + lax.rem(m, split)
        return remote(packed.at[m], block(rows, v), d_send.at[m], d_recv.at[m], ep=peer(m))

    def forward(v):
        m = pair_of(v)
        return remote(block(rows, v), block(rows, v), f_send.at[m], f_recv.at[m], ep=sibling)

    nexts = (z + 1, z - 1)
    prevs = (z - 1, z + 1)
    places = (z, depth - 1 - z)

    def chain(d, t):
        at = d * n + t
        return remote(part_out.at[at], part_in.at[at], c_send.at[at], c_recv.at[at], ctx=nexts[d])

    def spread(d, t):
        at = d * n + t
        return remote(hid.at[at], hid.at[at], b_send.at[at], b_recv.at[at], ctx=prevs[d])

    def swap(v):
        m = pair_of(v)
        return remote(block(half_out, v), half_in.at[m], h_send.at[m], h_recv.at[m], ep=sibling)

    def back(m):
        h = lax.rem(m, split)
        return remote(
            summed.at[m], ret_ref.at[chip * split + h], r_send.at[m], r_recv.at[chip * split + h], ep=peer(m)
        )

    def home(m):
        return remote(summed.at[m], ret_ref.at[m], r_send.at[m], r_recv.at[m], ep=peer(m))

    def share(o):
        other = lax.rem(z + o, depth)
        return remote(gat_ref.at[z], gat_ref.at[z], g_send.at[o], g_recv.at[o], ctx=other)

    def shared(o):
        other = lax.rem(z + depth - o, depth)
        return remote(gat_ref.at[z], gat_ref.at[other], g_send.at[o], g_recv.at[o], ctx=other)

    barrier = pltpu.get_barrier_semaphore()

    def greet(o, carry):
        pl.semaphore_signal(
            barrier, inc=1, device_id={"ep": 2 * flip(chip, o, chips) + core}, device_id_type=MESH
        )
        return carry

    lax.fori_loop(1, chips, greet, 0)
    pl.semaphore_signal(barrier, inc=1, device_id={"ep": sibling}, device_id_type=MESH)
    for o in range(1, depth):
        pl.semaphore_signal(
            barrier, inc=1, device_id={"ctx": lax.rem(z + o, depth)}, device_id_type=MESH
        )

    bf16, f32 = jnp.bfloat16, jnp.float32
    iota = lax.broadcasted_iota
    query_rows = query_ref.shape[0]
    lanes = gat_ref.shape[2]
    width_k = LAT + ROPE
    eye = iota(jnp.int32, (query_rows, query_rows), 0) == iota(jnp.int32, (query_rows, query_rows), 1)
    mark_col = jnp.sum(jnp.where(eye, mark_ref[...].astype(f32), 0.0), axis=1, keepdims=True)
    for o in range(1, depth):
        @pl.when(o > z)
        def _():
            gat_ref[o] = jnp.zeros((query_rows, lanes), bf16)

    gat_ref[z, :, :LAT] = lat_ref[...]
    gat_ref[z, :, LAT:width_k] = rope_ref[...]
    gat_ref[z, :, width_k:] = jnp.broadcast_to(mark_col, (query_rows, lanes - width_k)).astype(bf16)

    ids = ids_ref[...]
    tokens = ids.shape[1]
    kinds = max(chips, 16)
    named = iota(jnp.int32, (kinds, tokens), 0) == ids
    earlier = iota(jnp.int32, (tokens, tokens), 0) < iota(jnp.int32, (tokens, tokens), 1)
    counts = jnp.dot(
        jnp.where(named, 1.0, 0.0).astype(bf16),
        jnp.where(earlier, 1.0, 0.0).astype(bf16),
        preferred_element_type=f32,
    )
    rank = jnp.sum(jnp.where(named, counts, 0.0), axis=0, keepdims=True)
    slots = ids * cap + rank.astype(jnp.int32)

    pl.semaphore_wait(barrier, chips + depth - 1)
    for o in range(1, depth):
        @pl.when(z + o < depth)
        def _():
            share(o).start()

    def pack(o, carry):
        j = flip(chip, o, chips)
        index = j * cap + lax.broadcasted_iota(jnp.int32, (cap, tokens), 0)
        pick = jnp.where(index == slots, 1.0, 0.0).astype(jnp.bfloat16)
        chosen = jnp.dot(pick, feat_ref[...], preferred_element_type=jnp.float32)
        for h in range(split):
            packed[j * split + h] = chosen[h * unit:(h + 1) * unit].astype(bf16)

        @pl.when(o < 3)
        def _():
            for h in range(split):
                dispatch(j * split + h).start()

        return carry

    lax.fori_loop(1, chips, pack, 0)
    index = chip * cap + lax.broadcasted_iota(jnp.int32, (cap, tokens), 0)
    pick = jnp.where(index == slots, 1.0, 0.0).astype(jnp.bfloat16)
    chosen = jnp.dot(pick, feat_ref[...], preferred_element_type=jnp.float32)
    for h in range(split):
        block(rows, me * split + h)[...] = chosen[h * unit:(h + 1) * unit].astype(bf16)

    first = lax.div(me * split, group)
    lag = LAG * (depth - 1)

    heads = query_ref.shape[1] // width_k
    scale = 1.0 / math.sqrt(QK_DIM)

    def prepare():
        for o in range(1, depth):
            @pl.when(z >= o)
            def _():
                shared(o).wait_recv()

        count = depth * query_rows
        keys = gat_ref[...].reshape(count, lanes)
        row = iota(jnp.int32, (lanes, lanes), 0)
        column = iota(jnp.int32, (lanes, lanes), 1)
        even = (row == column) & (row < width_k)
        odd = row == column + (lanes - width_k)
        contract = (((1,), (1,)), ((), ()))
        for a, chosen in ((0, even), (1, odd)):
            pick = jnp.where(chosen, 1.0, 0.0).astype(bf16)
            keys_ref[a] = lax.dot_general(
                pick, keys, contract, preferred_element_type=f32
            ).astype(bf16)
        pick = jnp.where(iota(jnp.int32, (16, lanes), 1) == width_k, 1.0, 0.0).astype(bf16)
        marks = lax.dot_general(pick, keys, contract, preferred_element_type=f32)[:1]
        query_pos = z * query_rows + iota(jnp.int32, (query_rows, count), 0)
        key_pos = iota(jnp.int32, (query_rows, count), 1)
        visible = (key_pos == query_pos) | ((key_pos < query_pos) & (marks < 0.5))
        seen_ref[...] = jnp.where(visible, 0.0, -1e30)

    def attend_pair(pair):
        latents = gat_ref[:, :, :LAT].reshape(depth * query_rows, LAT)
        base = pl.multiple_of(pair * (2 * width_k), 128)
        mask = seen_ref[...]
        for a in range(2):
            shift = a * (2 * width_k - lanes)
            q = query_ref[:, pl.ds(pl.multiple_of(base + shift, 128), lanes)]
            scores = jnp.dot(q, keys_ref[a], preferred_element_type=f32) * scale
            masked = jnp.where(mask < 0.0, -1e30, scores)
            top = jnp.max(masked, axis=1, keepdims=True)
            weight = jnp.where(mask < 0.0, 0.0, jnp.exp(masked - top))
            total = jnp.sum(weight, axis=1, keepdims=True)
            acc = jnp.dot(weight.astype(bf16), latents, preferred_element_type=f32)
            where = pl.multiple_of((2 * pair + a) * LAT, 128)
            ctx_ref[:, pl.ds(where, LAT)] = (acc / total).astype(bf16)

    def step(i, carry):
        @pl.when(i == 1)
        def _():
            prepare()

        @pl.when((i >= 2) & (i < 2 + heads // 2))
        def _():
            attend_pair(i - 2)

        @pl.when(i == (FAR if chips == 4 else 0))
        def _():
            def far(o, carry):
                j = flip(chip, o, chips)
                for h in range(split):
                    dispatch(j * split + h).start()
                return carry

            lax.fori_loop(3, chips, far, 0)

        @pl.when(i < n)
        def _():
            q = flip(first, i, n)
            for g in range(group):
                v = q * group + g
                mine = core_of(v) == core

                @pl.when(mine & (lax.div(v, 2 * split) != chip))
                def _():
                    arrival(pair_of(v)).wait_recv()

                @pl.when(mine)
                def _():
                    forward(v).start()

            for g in range(group):
                v = q * group + g

                @pl.when(core_of(v) != core)
                def _():
                    forward(v).wait_recv()

        for d in range(2):
            t = i - LAG * places[d]
            lo, hi = d * quarter, (d + 1) * quarter

            @pl.when((t >= 0) & (t < n))
            def _():
                q = flip(first, t, n)
                at = d * n + t
                x = rows[q]
                gate = jnp.dot(x, gate_ref[:, lo:hi], preferred_element_type=jnp.float32)
                up = jnp.dot(x, up_ref[:, lo:hi], preferred_element_type=jnp.float32)

                @pl.when(places[d] == 0)
                def _():
                    part_out[at, :, :quarter] = gate.astype(jnp.bfloat16)
                    part_out[at, :, quarter:] = up.astype(jnp.bfloat16)
                    chain(d, t).start()

                @pl.when(places[d] > 0)
                def _():
                    chain(d, t).wait_recv()
                    gate_sum = gate + part_in[at, :, :quarter].astype(jnp.float32)
                    up_sum = up + part_in[at, :, quarter:].astype(jnp.float32)

                    @pl.when(places[d] < depth - 1)
                    def _():
                        part_out[at, :, :quarter] = gate_sum.astype(jnp.bfloat16)
                        part_out[at, :, quarter:] = up_sum.astype(jnp.bfloat16)
                        chain(d, t).start()

                    @pl.when(places[d] == depth - 1)
                    def _():
                        hid[at] = (jax.nn.silu(gate_sum) * up_sum).astype(jnp.bfloat16)
                        spread(d, t).start()

        for d in range(2):
            t = i - lag - LAG * (depth - 1 - places[d])

            @pl.when((t >= 0) & (t < n) & (places[d] < depth - 1))
            def _():
                spread(d, t).wait_recv()

                @pl.when(places[d] > 0)
                def _():
                    spread(d, t).start()

        t = i - 2 * lag

        @pl.when((t >= 0) & (t < n))
        def _():
            q = flip(first, t, n)
            h0 = hid[t]
            h1 = hid[n + t]
            tile = 256
            for w in range(0, width, tile):
                got = jnp.dot(h0, down_ref[:quarter, w:w + tile], preferred_element_type=jnp.float32)
                got = got + jnp.dot(
                    h1, down_ref[quarter:, w:w + tile], preferred_element_type=jnp.float32
                )
                half_out[q, :, w:w + tile] = got.astype(jnp.bfloat16)
            for g in range(group):
                v = q * group + g

                @pl.when(core_of(v) != core)
                def _():
                    swap(v).start()

        t2 = i - 2 * lag - split

        @pl.when((t2 >= 0) & (t2 < n))
        def _():
            q = flip(first, t2, n)
            for g in range(group):
                v = q * group + g
                m = pair_of(v)
                local = lax.div(m, split) == chip

                @pl.when(core_of(v) == core)
                def _():
                    swap(v).wait_recv()
                    total = block(half_out, v)[...].astype(f32) + half_in[m].astype(f32)
                    summed[m] = total.astype(bf16)

                    @pl.when(jnp.logical_not(local))
                    def _():
                        back(m).start()

                    @pl.when(local)
                    def _():
                        ret_ref[m] = total.astype(bf16)

        return carry

    lax.fori_loop(0, max(n + 2 * lag + split, 2 + heads // 2), step, 0)

    def land(o, carry):
        for h in range(split):
            home(flip(chip, o, chips) * split + h).wait_recv()
        return carry

    lax.fori_loop(1, chips, land, 0)
    diagonal = iota(jnp.int32, (tokens, tokens), 0) == iota(jnp.int32, (tokens, tokens), 1)
    slot_col = jnp.sum(jnp.where(diagonal, slots, 0), axis=1, keepdims=True)
    weight_col = jnp.sum(jnp.where(diagonal, weight_ref[...], 0.0), axis=1, keepdims=True)
    pick = jnp.where(iota(jnp.int32, (tokens, chips * cap), 1) == slot_col, 1.0, 0.0).astype(bf16)
    tile = 256
    for w in range(0, width, tile):
        mixed = jnp.dot(
            pick,
            ret_ref[:, :, w:w + tile].reshape(chips * cap, tile),
            preferred_element_type=f32,
        )
        moe_ref[:, w:w + tile] = (mixed * weight_col).astype(bf16)

    def finish(o, carry):
        j = flip(chip, o, chips)
        for h in range(split):
            dispatch(j * split + h).wait_send()
            back(j * split + h).wait_send()
        return carry

    lax.fori_loop(1, chips, finish, 0)

    def finish_core(j, carry):
        for h in range(split):
            forward((2 * j + core) * split + h).wait_send()
            swap((2 * j + 1 - core) * split + h).wait_send()
        return carry

    lax.fori_loop(0, chips, finish_core, 0)

    def finish_chain(t, carry):
        for d in range(2):
            @pl.when(places[d] < depth - 1)
            def _():
                chain(d, t).wait_send()

            @pl.when(places[d] > 0)
            def _():
                spread(d, t).wait_send()

        return carry

    lax.fori_loop(0, n, finish_chain, 0)
    for o in range(1, depth):
        @pl.when(z + o < depth)
        def _():
            share(o).wait_send()


def expert_call(ids, features, weight, w_gate, w_up, w_down, queries, latents, ropes, marks, chips, depth, cap):
    seq_len, width = features.shape
    hidden = w_gate.shape[1]
    split = max(1, CHUNKS // (2 * chips))
    group = 2 * chips * split // CHUNKS
    n = CHUNKS
    unit = cap // split
    tall = group * unit
    pairs = chips * split
    query_rows = queries.shape[0]
    heads = queries.shape[1] // (LAT + ROPE)
    lanes = -(-(LAT + ROPE + 1) // 128) * 128
    dma = pltpu.SemaphoreType.DMA
    bf16 = jnp.bfloat16
    vmem = pl.BlockSpec(memory_space=pltpu.VMEM)
    return pl.pallas_call(
        functools.partial(expert_kernel, chips, depth, cap, split, group),
        out_shape=(
            jax.ShapeDtypeStruct((seq_len, width), bf16),
            jax.ShapeDtypeStruct((query_rows, heads * LAT), bf16),
        ),
        in_specs=[vmem] * 10,
        out_specs=(vmem, vmem),
        scratch_shapes=[
            pltpu.VMEM((depth, query_rows, lanes), bf16),
            pltpu.VMEM((pairs, unit, width), bf16),
            pltpu.VMEM((2, lanes, depth * query_rows), bf16),
            pltpu.VMEM((query_rows, depth * query_rows), jnp.float32),
            pltpu.VMEM((pairs, unit, width), bf16),
            pltpu.VMEM((n, tall, width), bf16),
            pltpu.VMEM((2 * n, tall, hidden), bf16),
            pltpu.VMEM((2 * n, tall, hidden), bf16),
            pltpu.VMEM((2 * n, tall, hidden // 2), bf16),
            pltpu.VMEM((n, tall, width), bf16),
            pltpu.VMEM((pairs, unit, width), bf16),
            pltpu.VMEM((pairs, unit, width), bf16),
            dma((pairs,)), dma((pairs,)),
            dma((pairs,)), dma((pairs,)),
            dma((2 * n,)), dma((2 * n,)),
            dma((2 * n,)), dma((2 * n,)),
            dma((pairs,)), dma((pairs,)),
            dma((pairs,)), dma((pairs,)),
            dma((depth,)), dma((depth,)),
        ],
        compiler_params=pltpu.CompilerParams(
            collective_id=0, has_side_effects=True, vmem_limit_bytes=60 << 20
        ),
    )(ids, features, weight, w_gate, w_up, w_down, queries, latents, ropes, marks)


def per_device(
    hidden_in, expert_ids, route_weight, w_gate, w_up, w_down, queries, latents, rope_keys, marks
):
    features = hidden_in[0]
    seq_len = features.shape[0]
    slots_per = expert_ids.shape[2]
    chips = lax.axis_size("ep") // 2
    depth = lax.axis_size("ctx")
    capacity = max(2, 3 * seq_len * slots_per // (2 * chips))
    cap = -(-capacity // 16) * 16
    moe, context = expert_call(
        expert_ids[0].reshape(1, -1),
        features,
        route_weight[0].reshape(1, -1),
        w_gate,
        w_up,
        w_down,
        queries[0],
        latents[0],
        rope_keys[0],
        marks,
        chips,
        depth,
        cap,
    )
    return (moe[None], context[None])


def solution(mesh):
    placed = (
        P("ep", None, "ctx"),
        P("ep", None, None),
        P("ep", None, None),
        P("ctx", "ep"),
        P("ctx", "ep"),
        P("ep", "ctx"),
        P("ep", "ctx", None),
        P("ep", "ctx", None),
        P("ep", "ctx", None),
        P("ep", "ctx"),
    )
    return jax.shard_map(
        per_device,
        mesh=mesh,
        in_specs=placed,
        out_specs=(P("ep", None, "ctx"), P("ep", "ctx", None)),
        check_vma=False,
    )
```
